512 devices in a mesh: rep: 8 (over y, core), exp: 64 (over x, z).
Axes of the slice: x: 4, y: 4, z: 16, core: 2. Of those that a mesh axis runs over, the one named last changes fastest.
Arguments:
- tokens: bfloat16 [65536, 3584], P(('rep', 'exp')), may hold values from -6 to 6
- cotangent: bfloat16 [65536, 3584], P(('rep', 'exp')), may hold values from -0.29882812 to 0.29882812
- gates: float32 [65536, 1], P(('rep', 'exp')), may hold values from 0.2 to 1.5
- routes: int32 [65536, 1], P(('rep', 'exp')), may hold values from 0 to 15; in each aligned block of 128 rows (0 to 127, 128 to 255, ...) at most 9 rows name the same one
- w_up: bfloat16 [57344, 1024], P(('exp', 'rep')), may hold values from -0.09375 to 0.09375
- w_down_t: bfloat16 [57344, 1024], P(('exp', 'rep')), may hold values from -0.1875 to 0.1875
Outputs:
- grad_tokens: bfloat16 [65536, 3584], P(('rep', 'exp'))
- grad_gates: float32 [65536, 1], P(('rep', 'exp'))
- grad_up: float32 [57344, 1024], P(('exp', 'rep'))
- grad_down_t: float32 [57344, 1024], P(('exp', 'rep'))
The draws below stay inside these ranges and needn't reach their ends.
Inputs may be any that keep to these rules, and one draw needn't show every extreme that they name: `routes`: each row names one expert (1 = 1). Among the rows of one device no expert is named more than 9 times, and in every draw some expert is named exactly 9 times by the rows of some device.
All inputs are finite; a program needn't handle non-finite values.
Results may differ from the reference program's by a relative error of at most 0.012.
Values may be sent and summed in bfloat16 or wider, within the bound.
No kernel may reach another device: no remote copies, remote signals or barrier semaphores. Data moves between devices by JAX's collectives and lax.ppermute only.
A program may use at most 64 MiB of HBM per device.

```python
import math
import jax
import jax.numpy as jnp
import numpy as np
from jax import lax

D = 3584
HID = 1024
SLICES = 4
TOP = 1
TOK_DEV = 128
EXPERTS = 16
CAP = 9
TOKENS = 65536
N_REP = 8
N_EXP = 64


def levels(rng, dims, cuts, smallest, top_value):
    level, own = 1.0, jax.random.fold_in(rng, 6)
    for dim, blocks in cuts:
        steps = jnp.exp(jax.random.uniform(jax.random.fold_in(own, dim), (blocks,), jnp.float32, smallest / len(cuts), top_value / len(cuts)))
        level = level * jnp.repeat(steps, dims[dim] // blocks).reshape([-1 if axis == dim else 1 for axis in range(len(dims))])
    return level


def shared_out(own_key, own, number, rows, count, top, limit, slope):
    order = jax.random.permutation(own_key, count)
    crowded, usual = load_shares(count, rows * top, limit, slope, True), load_shares(count, rows * top, limit, slope, False)
    places = jnp.arange(count)

    def named(tallies, offset_by):
        used = int((tallies > 0).sum())
        fixed = max(1, used // 4)
        passed = fixed + (places - fixed + offset_by * (used - fixed)) % max(1, count - fixed)
        return jnp.zeros((count,), jnp.int32).at[order[jnp.where(places < fixed, places, passed)]].set(jnp.asarray(tallies, jnp.int32))

    tallies = jnp.where(number % 4 == 0, named(crowded, number // 4), named(usual, number - number // 4 - 1))
    mixed = jax.random.permutation(jax.random.fold_in(own, 3), count)
    source_of, receiver = mixed[0:count // 2 * 2:2], mixed[1:count // 2 * 2:2]
    margin = jnp.minimum(tallies[source_of] - 1, limit - tallies[receiver]) // 2
    margin = jnp.where((source_of == order[0]) | (receiver == order[0]) | (tallies[receiver] == 0), 0, jnp.maximum(margin, 0))
    passed = jax.random.randint(jax.random.fold_in(own, 4), (count // 2,), 0, 1 << 20) % (margin + 1)
    tallies = tallies.at[source_of].add(-passed).at[receiver].add(passed)
    members = jnp.searchsorted(jnp.cumsum(tallies), jnp.arange(rows * top), side="right").astype(jnp.int32)
    listing = members.reshape(top, rows).T
    listing = listing[jax.random.permutation(jax.random.fold_in(own, 1), rows)]
    offset_by = jax.random.randint(jax.random.fold_in(own, 2), (rows, 1), 0, top)
    return jnp.take_along_axis(listing, (jnp.arange(top)[None, :] + offset_by) % top, axis=1)


def load_shares(amount, total, limit, slope, full):
    portions = [(1 << 20) // math.isqrt(rank ** slope) + 1 for rank in range(1, amount + 1)]
    largest = limit if full else min(limit, max(-(-total // amount), total * portions[0] // sum(portions)))
    least = 1 if total - largest >= amount - 1 else 0
    given, rest = [largest] + [least] * (amount - 1), total - largest - least * (amount - 1)
    while rest > 0:
        free = [i for i in range(1, amount) if given[i] < largest] or [i for i in range(1, amount) if given[i] < limit]
        mass, left = sum([portions[i] for i in free]), rest
        for i in free:
            more = min(limit - given[i], max(1, left * portions[i] // mass), rest)
            given[i] = given[i] + more
            rest = rest - more
    return np.array(given)


def scatter_about(rng, extent, deviation, bound, split=(), kind=jnp.bfloat16):
    entries = jax.random.normal(rng, extent, jnp.float32) * deviation
    if len(split) > 0:
        entries = levels(rng, extent, split, -0.22, 0.18) * entries
    return jnp.clip(entries, min=-bound, max=bound).astype(kind)


def setup_inputs(seed: int = 0) -> dict:
    keys = jax.random.split(jax.random.key(seed), 7)
    tokens = scatter_about(keys[0], (TOKENS, D), 1.0, 6.0, ((0, 512),))
    cotangent = scatter_about(keys[1], (TOKENS, D), 0.05, 0.29882812, ((0, 512),))
    gates = jnp.clip(0.2 + 1.3 * jax.random.uniform(keys[2], (TOKENS, TOP), jnp.float32) ** levels(keys[2], (TOKENS, TOP), ((0, 512),), -0.2, 0.2), 0.2, 1.5)
    routes_keys = jax.random.split(jax.random.fold_in(keys[3], 1), TOKENS // TOK_DEV)
    routes_turns = jax.random.permutation(jax.random.fold_in(keys[3], 3), TOKENS // TOK_DEV)
    routes = jax.vmap(lambda own, number: shared_out(jax.random.fold_in(keys[3], 2), own, number, TOK_DEV, EXPERTS, TOP, CAP, 2))(routes_keys, routes_turns).reshape((TOKENS, TOP))
    w_up = scatter_about(keys[4], (EXPERTS * D, HID), D ** -0.5, 0.09375, ((0, 512),))
    w_down_t = scatter_about(keys[5], (EXPERTS * D, HID), HID ** -0.5, 0.1875, ((0, 512),))
    return {"tokens": tokens, "cotangent": cotangent, "gates": gates, "routes": routes, "w_up": w_up, "w_down_t": w_down_t}


def slot_numbers(route_rows):
    flat_route = route_rows.reshape(-1)
    onehot = (flat_route[:, None] == jnp.arange(EXPERTS, dtype=jnp.int32)[None, :]).astype(jnp.int32)
    earlier = jnp.cumsum(onehot, axis=0) - onehot
    return jnp.sum(earlier * onehot, axis=1).astype(jnp.int32)


def block_sum(left_side, right_side):
    piece_width = D // SLICES
    total = jnp.zeros((left_side.shape[0], right_side.shape[1]), jnp.float32)
    for slice_number in range(SLICES):
        lower = slice_number * piece_width
        upper = lower + piece_width
        part = jnp.dot(left_side[:, lower:upper], right_side[lower:upper], preferred_element_type=jnp.float32).astype(jnp.bfloat16)
        total = total + lax.optimization_barrier(part).astype(jnp.float32)
    return total


def reference(tokens, cotangent, gates, routes, w_up, w_down_t):
    group_rows = N_EXP * TOK_DEV
    choice_count = group_rows * TOP
    slot_total = N_EXP * CAP
    token_blocks = tokens.reshape(N_REP, group_rows, D)
    cot_blocks = cotangent.reshape(N_REP, group_rows, D)
    gate_blocks = gates.reshape(N_REP, group_rows, TOP)
    route_blocks = routes.reshape(N_REP, group_rows, TOP)

    def replica_step(carry, inputs):
        up_total, down_total = carry
        block_tokens, block_cot, block_gates, block_routes = inputs
        flat_route = block_routes.reshape(-1)
        slot_index = jax.vmap(slot_numbers)(block_routes.reshape(N_EXP, TOK_DEV * TOP)).reshape(-1)
        choice_ids = jnp.arange(choice_count, dtype=jnp.int32)
        source_dev = choice_ids // (TOK_DEV * TOP)
        position = (source_dev * CAP + slot_index).astype(jnp.int32)
        flat_gates = block_gates.reshape(-1)
        repeated = jnp.repeat(block_cot, TOP, axis=0).astype(jnp.float32)
        gate_grad = jnp.zeros((choice_count,), jnp.float32)
        input_grad = jnp.zeros((choice_count, D), jnp.float32)
        up_parts = []
        down_parts = []
        for expert in range(EXPERTS):
            selected = flat_route == expert
            target = jnp.where(selected, position, slot_total).astype(jnp.int32)
            table = jnp.full((slot_total + 1,), -1, dtype=jnp.int32).at[target].set(choice_ids)[:slot_total]
            filled = table >= 0
            chosen = jnp.maximum(table, 0).astype(jnp.int32)
            source_row = (chosen // TOP).astype(jnp.int32)
            inputs_buf = jnp.where(filled[:, None], block_tokens[source_row], jnp.zeros((), block_tokens.dtype))
            weight = flat_gates[chosen]
            grads_buf = jnp.where(filled[:, None], weight[:, None] * block_cot[source_row].astype(jnp.float32), jnp.float32(0.0)).astype(jnp.bfloat16)
            up_matrix = w_up[expert * D:(expert + 1) * D]
            down_matrix = w_down_t[expert * D:(expert + 1) * D]
            activation = block_sum(inputs_buf, up_matrix)
            gating = jax.nn.sigmoid(activation)
            hidden_act = (activation * gating).astype(jnp.bfloat16)
            outputs = jnp.dot(hidden_act, down_matrix.T, preferred_element_type=jnp.float32).astype(jnp.bfloat16)
            hidden_grad = block_sum(grads_buf, down_matrix)
            act_grad = (hidden_grad * gating * (1.0 + activation * (1.0 - gating))).astype(jnp.bfloat16)
            input_part = jnp.dot(act_grad, up_matrix.T, preferred_element_type=jnp.float32).astype(jnp.bfloat16)
            up_parts.append(jnp.dot(inputs_buf.T, act_grad, preferred_element_type=jnp.float32).astype(jnp.bfloat16))
            down_parts.append(jnp.dot(grads_buf.T, hidden_act, preferred_element_type=jnp.float32).astype(jnp.bfloat16))
            lookup = jnp.where(selected, position, 0).astype(jnp.int32)
            picked = outputs[lookup].astype(jnp.float32)
            gate_grad = gate_grad + jnp.where(selected, jnp.sum(repeated * picked, axis=1), jnp.float32(0.0))
            input_grad = input_grad + jnp.where(selected[:, None], input_part[lookup].astype(jnp.float32), jnp.float32(0.0))
        up_total = up_total + jnp.concatenate(up_parts, axis=0).astype(jnp.float32)
        down_total = down_total + jnp.concatenate(down_parts, axis=0).astype(jnp.float32)
        token_grad = jnp.sum(input_grad.reshape(group_rows, TOP, D), axis=1).astype(jnp.bfloat16)
        return (up_total, down_total), (token_grad, gate_grad.reshape(group_rows, TOP))

    start = (jnp.zeros((EXPERTS * D, HID), jnp.float32), jnp.zeros((EXPERTS * D, HID), jnp.float32))
    (grad_up, grad_down_t), (token_grads, gate_grads) = lax.scan(replica_step, start, (token_blocks, cot_blocks, gate_blocks, route_blocks))
    return token_grads.reshape(TOKENS, D), gate_grads.reshape(TOKENS, TOP), grad_up, grad_down_t
```

```python
import jax
import jax.numpy as jnp
from jax import lax
from jax.sharding import PartitionSpec as P

SLICES = 4
LANES = 128


def contract(left, right, dims):
    return lax.dot_general(
        left, right, ((dims[0], dims[1]), ((), ())), preferred_element_type=jnp.float32
    )


def xor_permute(x, bits):
    return lax.ppermute(x, "exp", [(i, i ^ bits) for i in range(lax.axis_size("exp"))])


def split3(x):
    first = x.astype(jnp.bfloat16)
    rest = x - first.astype(jnp.float32)
    second = rest.astype(jnp.bfloat16)
    third = (rest - second.astype(jnp.float32)).astype(jnp.bfloat16)
    return first, second, third


def shards(tokens, cotangent, gates, routes, w_up, w_down_t):
    tok_dev, model_width = tokens.shape
    piece = model_width // SLICES
    tiles = piece // LANES
    n_dev = lax.axis_size("exp")
    experts = n_dev // SLICES
    slots = 8
    quarter = n_dev // SLICES
    hidden = w_up.shape[1]
    bf16, f32 = jnp.bfloat16, jnp.float32
    me = lax.axis_index("exp") % SLICES

    up = lax.all_gather(w_up, "rep", axis=0, tiled=True)
    down = lax.all_gather(w_down_t, "rep", axis=0, tiled=True)

    route = routes.reshape(-1)
    order = jnp.arange(tok_dev, dtype=jnp.int32)
    same = (route[:, None] == route[None, :]) & (order[None, :] < order[:, None])
    slot = jnp.sum(same.astype(jnp.int32), axis=1)
    main_pos = jnp.where(slot < slots, route * slots + slot, experts * slots + route)
    rows = experts * (slots + 1)
    pick = (main_pos[None, :] == jnp.arange(rows, dtype=jnp.int32)[:, None]).astype(bf16)

    def dispatch(values):
        table = contract(pick, values, ((1,), (0,))).astype(bf16)
        main = table[: experts * slots].reshape(experts, slots, SLICES, tiles, LANES)
        main = main.transpose(0, 2, 3, 1, 4).reshape(n_dev, tiles, slots, LANES)
        extra = table[experts * slots :].reshape(n_dev, 1, tiles, LANES)
        extra = jnp.pad(extra, ((0, 0), (0, 0), (0, slots - tiles), (0, 0)))
        return lax.all_to_all(
            jnp.concatenate([main, extra], axis=1), "exp", split_axis=0, concat_axis=0, tiled=True
        )

    def unpack(got):
        main = got[:, :tiles].transpose(0, 2, 1, 3).reshape(SLICES, quarter * slots, piece)
        extra = got[:, tiles, :tiles].reshape(SLICES, quarter, piece)
        both = jnp.concatenate([main, extra], axis=1)
        return [
            lax.dynamic_index_in_dim(both, me ^ d, axis=0, keepdims=False) for d in range(SLICES)
        ]

    def reduced(blocks, weights):
        parts = [
            contract(blocks[d], weights, ((1,), (0,))).astype(bf16) for d in range(1, SLICES)
        ]
        got = [xor_permute(parts[d - 1], d) for d in range(1, SLICES)]
        own = contract(blocks[0], weights, ((1,), (0,))).astype(bf16)
        total = own.astype(f32)
        for part in got:
            total = total + part.astype(f32)
        return total

    def gathered(block):
        return [block] + [xor_permute(block, d) for d in range(1, SLICES)]

    x_blocks = unpack(dispatch(tokens))
    out_grad = (gates * cotangent.astype(f32)).astype(bf16)
    d_blocks = unpack(dispatch(out_grad))

    activation = reduced(x_blocks, up)
    gating = jax.nn.sigmoid(activation)
    hidden_act = (activation * gating).astype(bf16)
    h_all = jnp.concatenate(gathered(hidden_act), axis=0)
    hidden_grad = reduced(d_blocks, down)
    act_grad = (hidden_grad * gating * (1.0 + activation * (1.0 - gating))).astype(bf16)
    dots = jnp.sum(hidden_act.astype(f32) * hidden_grad, axis=1)
    g_blocks = gathered(act_grad)
    g_all = jnp.concatenate(g_blocks, axis=0)

    down_term = contract(jnp.concatenate(d_blocks, axis=0), h_all, ((0,), (0,))).astype(bf16)
    grad_down_t = lax.psum_scatter(down_term, "rep", scatter_dimension=0, tiled=True).astype(f32)
    up_term = contract(jnp.concatenate(x_blocks, axis=0), g_all, ((0,), (0,))).astype(bf16)
    grad_up = lax.psum_scatter(up_term, "rep", scatter_dimension=0, tiled=True).astype(f32)

    dx = contract(g_all, up, ((1,), (1,))).astype(bf16)
    dx = dx.reshape(SLICES, quarter * (slots + 1), piece)
    dx = jnp.stack(
        [lax.dynamic_index_in_dim(dx, me ^ d, axis=0, keepdims=False) for d in range(SLICES)]
    )
    main = dx[:, : quarter * slots].reshape(n_dev, slots, tiles, LANES).transpose(0, 2, 1, 3)
    extra = dx[:, quarter * slots :].reshape(n_dev, 1, tiles, LANES)
    per_source = jnp.concatenate(
        [dots[: quarter * slots].reshape(quarter, slots), dots[quarter * slots :][:, None]], axis=1
    )
    packed = jnp.concatenate(split3(per_source), axis=1)
    packed = jnp.pad(packed, ((0, 0), (0, LANES - packed.shape[1])))
    own = (jnp.arange(SLICES, dtype=jnp.int32) == me)[:, None, None]
    spare = jnp.where(own, packed[None], jnp.zeros((), bf16)).reshape(n_dev, 1, 1, LANES)
    extra = jnp.concatenate([extra, spare], axis=2)
    back = lax.all_to_all(
        jnp.concatenate([main, extra], axis=1), "exp", split_axis=0, concat_axis=0, tiled=True
    )

    main = back[:, :tiles].reshape(experts, SLICES, tiles, slots, LANES)
    main = main.transpose(0, 3, 1, 2, 4).reshape(experts * slots, model_width)
    extra = back[:, tiles, :tiles].reshape(experts, model_width)
    table = jnp.concatenate([main, extra], axis=0)
    grad_tokens = contract(pick, table, ((0,), (0,))).astype(bf16)
    spare = back[:, tiles, tiles].astype(f32).reshape(experts, SLICES, LANES).sum(axis=1)
    spare = spare[:, : 3 * (slots + 1)].reshape(experts, 3, slots + 1).sum(axis=1)
    flat = jnp.concatenate([spare[:, :slots].reshape(-1), spare[:, slots]])
    hit = main_pos[:, None] == jnp.arange(rows, dtype=jnp.int32)[None, :]
    grad_gates = jnp.sum(jnp.where(hit, flat[None, :], 0.0), axis=1, keepdims=True) / gates
    return grad_tokens, grad_gates, grad_up, grad_down_t


def solution(mesh):
    token_spec, weight_spec = P(("rep", "exp"), None), P(("exp", "rep"), None)
    return jax.shard_map(
        shards,
        mesh=mesh,
        in_specs=(token_spec,) * 4 + (weight_spec,) * 2,
        out_specs=(token_spec, token_spec, weight_spec, weight_spec),
        check_vma=False,
    )
```

```python
import jax
import jax.numpy as jnp
from jax import lax
from jax.sharding import PartitionSpec as P

SLICES = 4
LANES = 128
BOTH = ("rep", "exp")


def contract(left, right, dims):
    return lax.dot_general(
        left, right, ((dims[0], dims[1]), ((), ())), preferred_element_type=jnp.float32
    )


def split3(x):
    first = x.astype(jnp.bfloat16)
    rest = x - first.astype(jnp.float32)
    second = rest.astype(jnp.bfloat16)
    third = (rest - second.astype(jnp.float32)).astype(jnp.bfloat16)
    return first, second, third


def moved(x, n_rep, n_exp, where):
    pairs = []
    for rep in range(n_rep):
        for exp in range(n_exp):
            y, core, base, far, near = rep // 2, rep % 2, exp // 4 * 4, exp // 2 % 2, exp % 2
            core, far, near = where(core, far, near)
            pairs.append((rep * n_exp + exp, (y * 2 + core) * n_exp + base + far * 2 + near))
    return lax.ppermute(x, BOTH, pairs)


def shards(tokens, cotangent, gates, routes, w_up, w_down_t):
    tok_dev, model_width = tokens.shape
    piece = model_width // SLICES
    tiles = piece // LANES
    n_rep, n_dev = lax.axis_size("rep"), lax.axis_size("exp")
    experts = n_dev // SLICES
    slots = 8
    quarter = n_dev // SLICES
    per_quarter = quarter * (slots + 1)
    hidden = w_up.shape[1]
    bf16, f32 = jnp.bfloat16, jnp.float32
    core, far, near = lax.axis_index("rep") % 2, lax.axis_index("exp") // 2 % 2, lax.axis_index("exp") % 2
    me = core * 2 + near
    y_groups = [list(range(first, n_rep, 2)) for first in range(2)]
    token_groups = [
        [
            (y * 2 + c) * n_dev + e * SLICES + h * 2 + b
            for e in range(experts)
            for c in range(2)
            for b in range(2)
        ]
        for y in range(n_rep // 2)
        for h in range(2)
    ]

    def routed(x):
        return lax.all_to_all(
            x, BOTH, split_axis=0, concat_axis=0, axis_index_groups=token_groups, tiled=True
        )

    def other_core(x):
        return moved(x, n_rep, n_dev, lambda c, h, b: (1 - c, h, b))

    def other_near(x):
        return moved(x, n_rep, n_dev, lambda c, h, b: (c, h, 1 - b))

    def weights(w):
        first = moved(w, n_rep, n_dev, lambda c, h, b: (h, c, b))
        second = moved(w, n_rep, n_dev, lambda c, h, b: (h, 1 - c, b))
        pair = jnp.where(
            far == 0,
            jnp.concatenate([first, second], axis=0),
            jnp.concatenate([second, first], axis=0),
        )
        return lax.all_gather(pair, "rep", axis=0, axis_index_groups=y_groups, tiled=True)

    up = weights(w_up)
    down = weights(w_down_t)

    route = routes.reshape(-1)
    order = jnp.arange(tok_dev, dtype=jnp.int32)
    same = (route[:, None] == route[None, :]) & (order[None, :] < order[:, None])
    slot = jnp.sum(same.astype(jnp.int32), axis=1)
    main_pos = jnp.where(slot < slots, route * slots + slot, experts * slots + route)
    rows = experts * (slots + 1)
    pick = (main_pos[None, :] == jnp.arange(rows, dtype=jnp.int32)[:, None]).astype(bf16)

    def packed_rows(values):
        table = contract(pick, values, ((1,), (0,))).astype(bf16)
        main = table[: experts * slots].reshape(experts, slots, SLICES, tiles, LANES)
        main = main.transpose(0, 2, 3, 1, 4).reshape(n_dev, tiles, slots, LANES)
        extra = table[experts * slots :].reshape(n_dev, 1, tiles, LANES)
        extra = jnp.pad(extra, ((0, 0), (0, 0), (0, slots - tiles), (0, 0)))
        return [main, extra]

    def unpack(got):
        main = got[:, :tiles].transpose(0, 2, 1, 3).reshape(SLICES, quarter * slots, piece)
        extra = got[:, tiles, :tiles].reshape(SLICES, quarter, piece)
        both = jnp.concatenate([main, extra], axis=1)
        blocks = [
            lax.dynamic_index_in_dim(both, me ^ d, axis=0, keepdims=False) for d in range(SLICES)
        ]
        return jnp.concatenate(blocks, axis=0)

    def reduced(rows_in, matrix):
        theirs = contract(rows_in[2 * per_quarter :], matrix, ((1,), (0,))).astype(bf16)
        theirs = other_core(theirs)
        mine = contract(rows_in[: 2 * per_quarter], matrix, ((1,), (0,)))
        mine = mine + theirs.astype(f32)
        passed = other_near(mine[per_quarter:].astype(bf16))
        return mine[:per_quarter] + passed.astype(f32)

    def gathered(block):
        pair = jnp.concatenate([block, other_near(block)], axis=0)
        return jnp.concatenate([pair, other_core(pair)], axis=0)

    out_grad = (gates * cotangent.astype(f32)).astype(bf16)
    got = routed(jnp.concatenate(packed_rows(tokens) + packed_rows(out_grad), axis=1))
    x_rows = unpack(got[:, : tiles + 1])
    d_rows = unpack(got[:, tiles + 1 :])

    activation = reduced(x_rows, up)
    hidden_grad = reduced(d_rows, down)
    gating = jax.nn.sigmoid(activation)
    hidden_act = (activation * gating).astype(bf16)
    h_all = gathered(hidden_act)
    act_grad = (hidden_grad * gating * (1.0 + activation * (1.0 - gating))).astype(bf16)
    dots = jnp.sum(hidden_act.astype(f32) * hidden_grad, axis=1)
    g_all = gathered(act_grad)

    dx = contract(g_all, up, ((1,), (1,))).astype(bf16).reshape(SLICES, per_quarter, piece)
    dx = jnp.stack(
        [lax.dynamic_index_in_dim(dx, me ^ d, axis=0, keepdims=False) for d in range(SLICES)]
    )
    main = dx[:, : quarter * slots].reshape(n_dev, slots, tiles, LANES).transpose(0, 2, 1, 3)
    extra = dx[:, quarter * slots :].reshape(n_dev, 1, tiles, LANES)
    per_source = jnp.concatenate(
        [dots[: quarter * slots].reshape(quarter, slots), dots[quarter * slots :][:, None]], axis=1
    )
    packed = jnp.concatenate(split3(per_source), axis=1)
    packed = jnp.pad(packed, ((0, 0), (0, LANES - packed.shape[1])))
    own = (jnp.arange(SLICES, dtype=jnp.int32) == me)[:, None, None]
    spare = jnp.where(own, packed[None], jnp.zeros((), bf16)).reshape(n_dev, 1, 1, LANES)
    spare = jnp.pad(spare, ((0, 0), (0, 0), (0, slots - tiles - 1), (0, 0)))
    extra = jnp.concatenate([extra, spare], axis=2)
    back = routed(jnp.concatenate([main, extra], axis=1))

    down_term = contract(d_rows, h_all, ((0,), (0,))).astype(bf16)
    up_term = contract(x_rows, g_all, ((0,), (0,))).astype(bf16)
    terms = lax.psum_scatter(
        jnp.concatenate([up_term, down_term], axis=1),
        "rep",
        scatter_dimension=0,
        axis_index_groups=y_groups,
        tiled=True,
    )
    part = terms.shape[0] // 2
    low, high = terms[:part], terms[part:]
    swap = far == 1
    sums = moved(jnp.where(swap, high, low), n_rep, n_dev, lambda c, h, b: (h, c, b)).astype(f32)
    sums = sums + moved(
        jnp.where(swap, low, high), n_rep, n_dev, lambda c, h, b: (1 - h, c, b)
    ).astype(f32)

    main = back[:, :tiles].reshape(experts, SLICES, tiles, slots, LANES)
    main = main.transpose(0, 3, 1, 2, 4).reshape(experts * slots, model_width)
    extra = back[:, tiles, :tiles].reshape(experts, model_width)
    table = jnp.concatenate([main, extra], axis=0)
    grad_tokens = contract(pick, table, ((0,), (0,))).astype(bf16)
    spare = back[:, tiles, tiles].astype(f32).reshape(experts, SLICES, LANES).sum(axis=1)
    spare = spare[:, : 3 * (slots + 1)].reshape(experts, 3, slots + 1).sum(axis=1)
    flat = jnp.concatenate([spare[:, :slots].reshape(-1), spare[:, slots]])
    hit = main_pos[:, None] == jnp.arange(rows, dtype=jnp.int32)[None, :]
    grad_gates = jnp.sum(jnp.where(hit, flat[None, :], 0.0), axis=1, keepdims=True) / gates
    return grad_tokens, grad_gates, sums[:, :hidden], sums[:, hidden:]


def solution(mesh):
    token_spec, weight_spec = P(("rep", "exp"), None), P(("exp", "rep"), None)
    return jax.shard_map(
        shards,
        mesh=mesh,
        in_specs=(token_spec,) * 4 + (weight_spec,) * 2,
        out_specs=(token_spec, token_spec, weight_spec, weight_spec),
        check_vma=False,
    )
```

```python
import jax
import jax.numpy as jnp
from jax import lax
from jax.sharding import PartitionSpec as P


SLICES = 4
LANES = 128
Z_BLOCKS = 4
BOTH = ("rep", "exp")


def contract(left, right, dims):
    return lax.dot_general(
        left, right, ((dims[0], dims[1]), ((), ())), preferred_element_type=jnp.float32
    )


def split3(x):
    first = x.astype(jnp.bfloat16)
    rest = x - first.astype(jnp.float32)
    second = rest.astype(jnp.bfloat16)
    third = (rest - second.astype(jnp.float32)).astype(jnp.bfloat16)
    return first, second, third


def moved(x, n_rep, n_exp, where):
    pairs = []
    for rep in range(n_rep):
        for exp in range(n_exp):
            y, core, base, far, near = rep // 2, rep % 2, exp // 4 * 4, exp // 2 % 2, exp % 2
            core, far, near = where(core, far, near)
            pairs.append((rep * n_exp + exp, (y * 2 + core) * n_exp + base + far * 2 + near))
    return lax.ppermute(x, BOTH, pairs)


def shards(tokens, cotangent, gates, routes, w_up, w_down_t):
    tok_dev, model_width = tokens.shape
    piece = model_width // SLICES
    tiles = piece // LANES
    n_rep, n_dev = lax.axis_size("rep"), lax.axis_size("exp")
    experts = n_dev // SLICES
    slots = 8
    quarter = n_dev // SLICES
    per_quarter = quarter * (slots + 1)
    hidden = w_up.shape[1]
    bf16, f32 = jnp.bfloat16, jnp.float32
    core, far, near = lax.axis_index("rep") % 2, lax.axis_index("exp") // 2 % 2, lax.axis_index("exp") % 2
    me = core * 2 + near
    y_groups = [list(range(first, n_rep, 2)) for first in range(2)]
    token_groups = [
        [
            (y * 2 + c) * n_dev + e * SLICES + (k ^ e % Z_BLOCKS // 2) * 2 + b
            for e in range(experts)
            for c in range(2)
            for b in range(2)
        ]
        for y in range(n_rep // 2)
        for k in range(2)
    ]

    def routed(x):
        return lax.all_to_all(
            x, BOTH, split_axis=0, concat_axis=0, axis_index_groups=token_groups, tiled=True
        )

    def other_core(x):
        return moved(x, n_rep, n_dev, lambda c, h, b: (1 - c, h, b))

    def other_near(x):
        return moved(x, n_rep, n_dev, lambda c, h, b: (c, h, 1 - b))

    def weights(w):
        first = moved(w, n_rep, n_dev, lambda c, h, b: (h, c, b))
        second = moved(w, n_rep, n_dev, lambda c, h, b: (h, 1 - c, b))
        pair = jnp.where(
            far == 0,
            jnp.concatenate([first, second], axis=0),
            jnp.concatenate([second, first], axis=0),
        )
        return lax.all_gather(pair, "rep", axis=0, axis_index_groups=y_groups, tiled=True)

    up = weights(w_up)
    down = weights(w_down_t)

    route = routes.reshape(-1)
    order = jnp.arange(tok_dev, dtype=jnp.int32)
    same = (route[:, None] == route[None, :]) & (order[None, :] < order[:, None])
    slot = jnp.sum(same.astype(jnp.int32), axis=1)
    main_pos = jnp.where(slot < slots, route * slots + slot, experts * slots + route)
    rows = experts * (slots + 1)
    pick = (main_pos[None, :] == jnp.arange(rows, dtype=jnp.int32)[:, None]).astype(bf16)

    def packed_rows(values):
        table = contract(pick, values, ((1,), (0,))).astype(bf16)
        main = table[: experts * slots].reshape(experts, slots, SLICES, tiles, LANES)
        main = main.transpose(0, 2, 3, 1, 4).reshape(n_dev, tiles, slots, LANES)
        extra = table[experts * slots :].reshape(n_dev, 1, tiles, LANES)
        extra = jnp.pad(extra, ((0, 0), (0, 0), (0, slots - tiles), (0, 0)))
        return [main, extra]

    def unpack(got):
        main = got[:, :tiles].transpose(0, 2, 1, 3).reshape(SLICES, quarter * slots, piece)
        extra = got[:, tiles, :tiles].reshape(SLICES, quarter, piece)
        both = jnp.concatenate([main, extra], axis=1)
        blocks = [
            lax.dynamic_index_in_dim(both, me ^ d, axis=0, keepdims=False) for d in range(SLICES)
        ]
        return jnp.concatenate(blocks, axis=0)

    def reduced(rows_in, matrix):
        theirs = contract(rows_in[2 * per_quarter :], matrix, ((1,), (0,))).astype(bf16)
        theirs = other_core(theirs)
        mine = contract(rows_in[: 2 * per_quarter], matrix, ((1,), (0,)))
        mine = mine + theirs.astype(f32)
        passed = other_near(mine[per_quarter:].astype(bf16))
        return mine[:per_quarter] + passed.astype(f32)

    def gathered(block):
        pair = jnp.concatenate([block, other_near(block)], axis=0)
        return jnp.concatenate([pair, other_core(pair)], axis=0)

    out_grad = (gates * cotangent.astype(f32)).astype(bf16)
    sent = jnp.concatenate(packed_rows(tokens) + packed_rows(out_grad), axis=1)
    got = routed(sent)
    x_rows = unpack(got[:, : tiles + 1])
    d_rows = unpack(got[:, tiles + 1 :])

    activation = reduced(x_rows, up)
    hidden_grad = reduced(d_rows, down)
    gating = jax.nn.sigmoid(activation)
    hidden_act = (activation * gating).astype(bf16)
    h_all = gathered(hidden_act)
    act_grad = (hidden_grad * gating * (1.0 + activation * (1.0 - gating))).astype(bf16)
    dots = jnp.sum(hidden_act.astype(f32) * hidden_grad, axis=1)
    g_all = gathered(act_grad)

    dx = contract(g_all, up, ((1,), (1,))).astype(bf16).reshape(SLICES, per_quarter, piece)
    dx = jnp.stack(
        [lax.dynamic_index_in_dim(dx, me ^ d, axis=0, keepdims=False) for d in range(SLICES)]
    )
    main = dx[:, : quarter * slots].reshape(n_dev, slots, tiles, LANES).transpose(0, 2, 1, 3)
    extra = dx[:, quarter * slots :].reshape(n_dev, 1, tiles, LANES)
    per_source = jnp.concatenate(
        [dots[: quarter * slots].reshape(quarter, slots), dots[quarter * slots :][:, None]], axis=1
    )
    packed = jnp.concatenate(split3(per_source), axis=1)
    packed = jnp.pad(packed, ((0, 0), (0, LANES - packed.shape[1])))
    own = (jnp.arange(SLICES, dtype=jnp.int32) == me)[:, None, None]
    spare = jnp.where(own, packed[None], jnp.zeros((), bf16)).reshape(n_dev, 1, 1, LANES)
    spare = jnp.pad(spare, ((0, 0), (0, 0), (0, slots - tiles - 1), (0, 0)))
    extra = jnp.concatenate([extra, spare], axis=2)
    sent = jnp.concatenate([main, extra], axis=1)
    back = routed(sent)

    down_term = contract(d_rows, h_all, ((0,), (0,))).astype(bf16)
    up_term = contract(x_rows, g_all, ((0,), (0,))).astype(bf16)
    terms = lax.psum_scatter(
        jnp.concatenate([up_term, down_term], axis=1),
        "rep",
        scatter_dimension=0,
        axis_index_groups=y_groups,
        tiled=True,
    )
    part = terms.shape[0] // 2
    low, high = terms[:part], terms[part:]
    swap = far == 1
    first, second = jnp.where(swap, high, low), jnp.where(swap, low, high)
    first = moved(first, n_rep, n_dev, lambda c, h, b: (h, c, b))
    second = moved(second, n_rep, n_dev, lambda c, h, b: (1 - h, c, b))
    sums = first.astype(f32) + second.astype(f32)

    main = back[:, :tiles].reshape(experts, SLICES, tiles, slots, LANES)
    main = main.transpose(0, 3, 1, 2, 4).reshape(experts * slots, model_width)
    extra = back[:, tiles, :tiles].reshape(experts, model_width)
    table = jnp.concatenate([main, extra], axis=0)
    grad_tokens = contract(pick, table, ((0,), (0,))).astype(bf16)
    spare = back[:, tiles, tiles].astype(f32).reshape(experts, SLICES, LANES).sum(axis=1)
    spare = spare[:, : 3 * (slots + 1)].reshape(experts, 3, slots + 1).sum(axis=1)
    flat = jnp.concatenate([spare[:, :slots].reshape(-1), spare[:, slots]])
    hit = main_pos[:, None] == jnp.arange(rows, dtype=jnp.int32)[None, :]
    grad_gates = jnp.sum(jnp.where(hit, flat[None, :], 0.0), axis=1, keepdims=True) / gates
    return grad_tokens, grad_gates, sums[:, :hidden], sums[:, hidden:]


def solution(mesh):
    token_spec, weight_spec = P(("rep", "exp"), None), P(("exp", "rep"), None)
    return jax.shard_map(
        shards,
        mesh=mesh,
        in_specs=(token_spec,) * 4 + (weight_spec,) * 2,
        out_specs=(token_spec, token_spec, weight_spec, weight_spec),
        check_vma=False,
    )
```

```python
import jax
import jax.numpy as jnp
from jax import lax
from jax.sharding import PartitionSpec as P


SLICES = 4
LANES = 128
Z_BLOCKS = 4
BOTH = ("rep", "exp")


def contract(left, right, dims):
    return lax.dot_general(
        left, right, ((dims[0], dims[1]), ((), ())), preferred_element_type=jnp.float32
    )


def split3(x):
    first = x.astype(jnp.bfloat16)
    rest = x - first.astype(jnp.float32)
    second = rest.astype(jnp.bfloat16)
    third = (rest - second.astype(jnp.float32)).astype(jnp.bfloat16)
    return first, second, third


def moved(x, n_rep, n_exp, where, shift=0):
    pairs = []
    for rep in range(n_rep):
        for exp in range(n_exp):
            y, core, base, far, near = rep // 2, rep % 2, exp // 4 * 4, exp // 2 % 2, exp % 2
            core, far, near = where(core, far, near)
            y = (y + shift) % (n_rep // 2)
            pairs.append((rep * n_exp + exp, (y * 2 + core) * n_exp + base + far * 2 + near))
    return lax.ppermute(x, BOTH, pairs)


def shards(tokens, cotangent, gates, routes, w_up, w_down_t):
    tok_dev, model_width = tokens.shape
    piece = model_width // SLICES
    tiles = piece // LANES
    n_rep, n_dev = lax.axis_size("rep"), lax.axis_size("exp")
    experts = n_dev // SLICES
    slots = 8
    quarter = n_dev // SLICES
    per_quarter = quarter * (slots + 1)
    bf16, f32 = jnp.bfloat16, jnp.float32
    core, far, near = lax.axis_index("rep") % 2, lax.axis_index("exp") // 2 % 2, lax.axis_index("exp") % 2
    me = core * 2 + near
    token_groups = [
        [
            (y * 2 + c) * n_dev + e * SLICES + (k ^ e % Z_BLOCKS // 2) * 2 + b
            for e in range(experts)
            for c in range(2)
            for b in range(2)
        ]
        for y in range(n_rep // 2)
        for k in range(2)
    ]

    y_now, y_size = lax.axis_index("rep") // 2, n_rep // 2

    def ring(x, step):
        return moved(x, n_rep, n_dev, lambda c, h, b: (c, h, b), step)

    def gathered_weights(own_up, own_down):
        own = jnp.concatenate([own_up, own_down], axis=0)
        half = own_up.shape[0]
        left, right = ring(own, 1), ring(own, -1)
        far_up, far_down = ring(left[:half], 1), ring(right[half:], -1)

        def placed(blocks):
            twice = jnp.concatenate(blocks + blocks, axis=0)
            start = (y_size - y_now) * half
            return lax.dynamic_slice_in_dim(twice, start, y_size * half, axis=0)

        return (
            placed([own_up, right[:half], far_up, left[:half]]),
            placed([own_down, right[half:], far_down, left[half:]]),
        )

    def replica_sum(term, shift):
        rows_y, cols = term.shape[0] // y_size, term.shape[1] // 2

        def block(step):
            start = (y_now + shift + step + y_size) % y_size * rows_y
            return lax.dynamic_slice_in_dim(term, start, rows_y, axis=0)

        def plus(part, got):
            return (part.astype(f32) + got.astype(f32)).astype(bf16)

        across = block(2)
        from_left = ring(across[:, :cols], 1)
        from_right = ring(across[:, cols:], -1)
        ahead, behind = block(1), block(3)
        ahead = jnp.concatenate([plus(ahead[:, :cols], from_left), ahead[:, cols:]], axis=1)
        behind = jnp.concatenate([behind[:, :cols], plus(behind[:, cols:], from_right)], axis=1)
        from_left, from_right = ring(ahead, 1), ring(behind, -1)
        total = block(0).astype(f32) + from_left.astype(f32) + from_right.astype(f32)
        total = total.astype(bf16)
        low, high = total[: rows_y // 2], total[rows_y // 2 :]
        first, second = jnp.where(far == 1, high, low), jnp.where(far == 1, low, high)
        first = moved(first, n_rep, n_dev, lambda c, h, b: (h, c, b), shift)
        second = moved(second, n_rep, n_dev, lambda c, h, b: (1 - h, c, b), shift)
        return first.astype(f32) + second.astype(f32)

    def routed(x):
        return lax.all_to_all(
            x, BOTH, split_axis=0, concat_axis=0, axis_index_groups=token_groups, tiled=True
        )

    def other_core(x):
        return moved(x, n_rep, n_dev, lambda c, h, b: (1 - c, h, b))

    def other_near(x):
        return moved(x, n_rep, n_dev, lambda c, h, b: (c, h, 1 - b))

    both = jnp.concatenate([w_up, w_down_t], axis=0)
    first = moved(both, n_rep, n_dev, lambda c, h, b: (h, c, b))
    second = moved(both, n_rep, n_dev, lambda c, h, b: (h, 1 - c, b))
    part = w_up.shape[0]

    def paired(rows):
        ones, twos = first[rows], second[rows]
        return jnp.where(
            far == 0, jnp.concatenate([ones, twos], axis=0), jnp.concatenate([twos, ones], axis=0)
        )

    own_up = paired(slice(0, part))
    own_down = paired(slice(part, 2 * part))
    up, down = gathered_weights(own_up, own_down)

    route = routes.reshape(-1)
    order = jnp.arange(tok_dev, dtype=jnp.int32)
    same = (route[:, None] == route[None, :]) & (order[None, :] < order[:, None])
    slot = jnp.sum(same.astype(jnp.int32), axis=1)
    main_pos = jnp.where(slot < slots, route * slots + slot, experts * slots + route)
    rows = experts * (slots + 1)
    pick = (main_pos[None, :] == jnp.arange(rows, dtype=jnp.int32)[:, None]).astype(bf16)

    def packed_rows(values):
        table = contract(pick, values, ((1,), (0,))).astype(bf16)
        main = table[: experts * slots].reshape(experts, slots, SLICES, tiles, LANES)
        main = main.transpose(0, 2, 3, 1, 4).reshape(n_dev, tiles, slots, LANES)
        extra = table[experts * slots :].reshape(n_dev, 1, tiles, LANES)
        extra = jnp.pad(extra, ((0, 0), (0, 0), (0, slots - tiles), (0, 0)))
        return [main, extra]

    def unpack(got):
        main = got[:, :tiles].transpose(0, 2, 1, 3).reshape(SLICES, quarter * slots, piece)
        extra = got[:, tiles, :tiles].reshape(SLICES, quarter, piece)
        both = jnp.concatenate([main, extra], axis=1)
        blocks = [
            lax.dynamic_index_in_dim(both, me ^ d, axis=0, keepdims=False) for d in range(SLICES)
        ]
        return jnp.concatenate(blocks, axis=0)

    def reduced(rows_in, matrix):
        theirs = contract(rows_in[2 * per_quarter :], matrix, ((1,), (0,))).astype(bf16)
        theirs = other_core(theirs)
        mine = contract(rows_in[: 2 * per_quarter], matrix, ((1,), (0,)))
        mine = mine + theirs.astype(f32)
        ours = mine.astype(bf16)
        passed = other_near(ours)
        passed = jnp.concatenate([passed[per_quarter:], passed[:per_quarter]], axis=0)
        return ours.astype(f32) + passed.astype(f32)

    def gathered(pair):
        return jnp.concatenate([pair, other_core(pair)], axis=0)

    out_grad = (gates * cotangent.astype(f32)).astype(bf16)
    sent = jnp.concatenate(packed_rows(tokens) + packed_rows(out_grad), axis=1)
    got = routed(sent)
    x_rows = unpack(got[:, : tiles + 1])
    d_rows = unpack(got[:, tiles + 1 :])

    activation = reduced(x_rows, up)
    hidden_grad = reduced(d_rows, down)
    gating = jax.nn.sigmoid(activation)
    hidden_act = (activation * gating).astype(bf16)
    hidden_act, activation = lax.optimization_barrier((hidden_act, activation))
    gating = jax.nn.sigmoid(activation)
    h_all = gathered(hidden_act)
    down_term = contract(d_rows, h_all, ((0,), (0,))).astype(bf16)
    act_grad = (hidden_grad * gating * (1.0 + activation * (1.0 - gating))).astype(bf16)
    dots = jnp.sum((hidden_act.astype(f32) * hidden_grad)[:per_quarter], axis=1)
    g_all = gathered(act_grad)

    dx = contract(g_all, up, ((1,), (1,))).astype(bf16).reshape(SLICES, per_quarter, piece)
    dx = jnp.stack(
        [lax.dynamic_index_in_dim(dx, me ^ d, axis=0, keepdims=False) for d in range(SLICES)]
    )
    main = dx[:, : quarter * slots].reshape(n_dev, slots, tiles, LANES).transpose(0, 2, 1, 3)
    extra = dx[:, quarter * slots :].reshape(n_dev, 1, tiles, LANES)
    per_source = jnp.concatenate(
        [dots[: quarter * slots].reshape(quarter, slots), dots[quarter * slots :][:, None]], axis=1
    )
    packed = jnp.concatenate(split3(per_source), axis=1)
    packed = jnp.pad(packed, ((0, 0), (0, LANES - packed.shape[1])))
    own = (jnp.arange(SLICES, dtype=jnp.int32) == me)[:, None, None]
    spare = jnp.where(own, packed[None], jnp.zeros((), bf16)).reshape(n_dev, 1, 1, LANES)
    spare = jnp.pad(spare, ((0, 0), (0, 0), (0, slots - tiles - 1), (0, 0)))
    extra = jnp.concatenate([extra, spare], axis=2)
    sent = jnp.concatenate([main, extra], axis=1)
    back = routed(sent)

    up_term = contract(x_rows, g_all, ((0,), (0,))).astype(bf16)
    grad_down_t = replica_sum(down_term, -1)
    grad_up = replica_sum(up_term, 1)

    main = back[:, :tiles].reshape(experts, SLICES, tiles, slots, LANES)
    main = main.transpose(0, 3, 1, 2, 4).reshape(experts * slots, model_width)
    extra = back[:, tiles, :tiles].reshape(experts, model_width)
    table = jnp.concatenate([main, extra], axis=0)
    grad_tokens = contract(pick, table, ((0,), (0,))).astype(bf16)
    spare = back[:, tiles, tiles].astype(f32).reshape(experts, SLICES, LANES).sum(axis=1)
    spare = spare[:, : 3 * (slots + 1)].reshape(experts, 3, slots + 1).sum(axis=1)
    flat = jnp.concatenate([spare[:, :slots].reshape(-1), spare[:, slots]])
    hit = main_pos[:, None] == jnp.arange(rows, dtype=jnp.int32)[None, :]
    grad_gates = jnp.sum(jnp.where(hit, flat[None, :], 0.0), axis=1, keepdims=True) / gates
    return grad_tokens, grad_gates, grad_up, grad_down_t


def solution(mesh):
    token_spec, weight_spec = P(("rep", "exp"), None), P(("exp", "rep"), None)
    return jax.shard_map(
        shards,
        mesh=mesh,
        in_specs=(token_spec,) * 4 + (weight_spec,) * 2,
        out_specs=(token_spec, token_spec, weight_spec, weight_spec),
        check_vma=False,
    )
```

```python
import jax
import jax.numpy as jnp
from jax import lax
from jax.sharding import PartitionSpec as P


SLICES = 4
LANES = 128
Z_BLOCKS = 4
BOTH = ("rep", "exp")


def contract(left, right, dims):
    return lax.dot_general(
        left, right, ((dims[0], dims[1]), ((), ())), preferred_element_type=jnp.float32
    )


def split3(x):
    first = x.astype(jnp.bfloat16)
    rest = x - first.astype(jnp.float32)
    second = rest.astype(jnp.bfloat16)
    third = (rest - second.astype(jnp.float32)).astype(jnp.bfloat16)
    return first, second, third


def moved(x, n_rep, n_exp, where, shift=0):
    pairs = []
    for rep in range(n_rep):
        for exp in range(n_exp):
            y, core, base, far, near = rep // 2, rep % 2, exp // 4 * 4, exp // 2 % 2, exp % 2
            core, far, near = where(core, far, near)
            y = (y + shift) % (n_rep // 2)
            pairs.append((rep * n_exp + exp, (y * 2 + core) * n_exp + base + far * 2 + near))
    return lax.ppermute(x, BOTH, pairs)


def shards(tokens, cotangent, gates, routes, w_up, w_down_t):
    tok_dev, model_width = tokens.shape
    piece = model_width // SLICES
    tiles = piece // LANES
    n_rep, n_dev = lax.axis_size("rep"), lax.axis_size("exp")
    experts = n_dev // SLICES
    slots = 8
    quarter = n_dev // SLICES
    per_quarter = quarter * (slots + 1)
    hidden = w_up.shape[1]
    bf16, f32 = jnp.bfloat16, jnp.float32
    core, far, near = lax.axis_index("rep") % 2, lax.axis_index("exp") // 2 % 2, lax.axis_index("exp") % 2
    me = core * 2 + near
    token_groups = [
        [
            (y * 2 + c) * n_dev + e * SLICES + (k ^ e % Z_BLOCKS // 2) * 2 + b
            for e in range(experts)
            for c in range(2)
            for b in range(2)
        ]
        for y in range(n_rep // 2)
        for k in range(2)
    ]

    y_now, y_size = lax.axis_index("rep") // 2, n_rep // 2

    def ring(x, step):
        return moved(x, n_rep, n_dev, lambda c, h, b: (c, h, b), step)

    def gathered_weights(own_up, own_down):
        own = jnp.concatenate([own_up, own_down], axis=0)
        half = own_up.shape[0]
        left, right = ring(own, 1), ring(own, -1)
        far_up, far_down = ring(left[:half], 1), ring(right[half:], -1)

        def placed(blocks):
            twice = jnp.concatenate(blocks + blocks, axis=0)
            start = (y_size - y_now) * half
            return lax.dynamic_slice_in_dim(twice, start, y_size * half, axis=0)

        return (
            placed([own_up, right[:half], far_up, left[:half]]),
            placed([own_down, right[half:], far_down, left[half:]]),
        )

    def y_block(term, step):
        rows_y = term.shape[0] // y_size
        start = (y_now + 1 + step) % y_size * rows_y
        return lax.dynamic_slice_in_dim(term, start, rows_y, axis=0)

    def plus(part, got):
        return (part.astype(f32) + got.astype(f32)).astype(bf16)

    def replica_sum(up_term, down_term, got_up, got_down):
        ahead = jnp.concatenate([plus(y_block(up_term, 1), got_up), y_block(down_term, 1)], axis=1)
        behind = jnp.concatenate(
            [y_block(up_term, 3), plus(y_block(down_term, 3), got_down)], axis=1
        )
        from_left, from_right = ring(ahead, 1), ring(behind, -1)
        total = jnp.concatenate([y_block(up_term, 0), y_block(down_term, 0)], axis=1).astype(f32)
        total = (total + from_left.astype(f32) + from_right.astype(f32)).astype(bf16)
        half = total.shape[0] // 2
        low, high = total[:half], total[half:]
        first, second = jnp.where(far == 1, high, low), jnp.where(far == 1, low, high)
        first = moved(first, n_rep, n_dev, lambda c, h, b: (h, c, b), 1)
        second = moved(second, n_rep, n_dev, lambda c, h, b: (1 - h, c, b), 1)
        return first.astype(f32) + second.astype(f32)

    def routed(x):
        return lax.all_to_all(
            x, BOTH, split_axis=0, concat_axis=0, axis_index_groups=token_groups, tiled=True
        )

    def other_core(x):
        return moved(x, n_rep, n_dev, lambda c, h, b: (1 - c, h, b))

    def other_near(x):
        return moved(x, n_rep, n_dev, lambda c, h, b: (c, h, 1 - b))

    both = jnp.concatenate([w_up, w_down_t], axis=0)
    first = moved(both, n_rep, n_dev, lambda c, h, b: (h, c, b))
    second = moved(both, n_rep, n_dev, lambda c, h, b: (h, 1 - c, b))
    part = w_up.shape[0]

    def paired(rows):
        ones, twos = first[rows], second[rows]
        return jnp.where(
            far == 0, jnp.concatenate([ones, twos], axis=0), jnp.concatenate([twos, ones], axis=0)
        )

    own_up = paired(slice(0, part))
    own_down = paired(slice(part, 2 * part))
    up, down = gathered_weights(own_up, own_down)

    route = routes.reshape(-1)
    order = jnp.arange(tok_dev, dtype=jnp.int32)
    same = (route[:, None] == route[None, :]) & (order[None, :] < order[:, None])
    slot = jnp.sum(same.astype(jnp.int32), axis=1)
    main_pos = jnp.where(slot < slots, route * slots + slot, experts * slots + route)
    rows = experts * (slots + 1)
    pick = (main_pos[None, :] == jnp.arange(rows, dtype=jnp.int32)[:, None]).astype(bf16)

    def packed_rows(values):
        table = contract(pick, values, ((1,), (0,))).astype(bf16)
        main = table[: experts * slots].reshape(experts, slots, SLICES, tiles, LANES)
        main = main.transpose(0, 2, 3, 1, 4).reshape(n_dev, tiles, slots, LANES)
        extra = table[experts * slots :].reshape(n_dev, 1, tiles, LANES)
        extra = jnp.pad(extra, ((0, 0), (0, 0), (0, slots - tiles), (0, 0)))
        return [main, extra]

    def unpack(got):
        main = got[:, :tiles].transpose(0, 2, 1, 3).reshape(SLICES, quarter * slots, piece)
        extra = got[:, tiles, :tiles].reshape(SLICES, quarter, piece)
        both = jnp.concatenate([main, extra], axis=1)
        blocks = [
            lax.dynamic_index_in_dim(both, me ^ d, axis=0, keepdims=False) for d in range(SLICES)
        ]
        return jnp.concatenate(blocks, axis=0)

    def reduced(rows_in, matrix):
        theirs = contract(rows_in[2 * per_quarter :], matrix, ((1,), (0,))).astype(bf16)
        theirs = other_core(theirs)
        mine = contract(rows_in[: 2 * per_quarter], matrix, ((1,), (0,)))
        ours = (mine + theirs.astype(f32)).astype(bf16)
        passed = other_near(ours)
        passed = jnp.concatenate([passed[per_quarter:], passed[:per_quarter]], axis=0)
        return ours.astype(f32) + passed.astype(f32)

    def gathered(pair):
        return jnp.concatenate([pair, other_core(pair)], axis=0)

    out_grad = (gates * cotangent.astype(f32)).astype(bf16)
    sent = jnp.concatenate(packed_rows(tokens) + packed_rows(out_grad), axis=1)
    got = routed(sent)
    x_rows = unpack(got[:, : tiles + 1])
    d_rows = unpack(got[:, tiles + 1 :])

    activation = reduced(x_rows, up)
    hidden_grad = reduced(d_rows, down)
    gating = jax.nn.sigmoid(activation)
    hidden_act = (activation * gating).astype(bf16)
    hidden_act, activation = lax.optimization_barrier((hidden_act, activation))
    gating = jax.nn.sigmoid(activation)
    h_all = gathered(hidden_act)
    down_term = contract(d_rows, h_all, ((0,), (0,))).astype(bf16)
    got_down = ring(y_block(down_term, 2), -1)
    act_grad = (hidden_grad * gating * (1.0 + activation * (1.0 - gating))).astype(bf16)
    dots = jnp.sum((hidden_act.astype(f32) * hidden_grad)[:per_quarter], axis=1)
    g_all = gathered(act_grad)

    dx = contract(g_all, up, ((1,), (1,))).astype(bf16).reshape(SLICES, per_quarter, piece)
    dx = jnp.stack(
        [lax.dynamic_index_in_dim(dx, me ^ d, axis=0, keepdims=False) for d in range(SLICES)]
    )
    main = dx[:, : quarter * slots].reshape(n_dev, slots, tiles, LANES).transpose(0, 2, 1, 3)
    extra = dx[:, quarter * slots :].reshape(n_dev, 1, tiles, LANES)
    per_source = jnp.concatenate(
        [dots[: quarter * slots].reshape(quarter, slots), dots[quarter * slots :][:, None]], axis=1
    )
    packed = jnp.concatenate(split3(per_source), axis=1)
    packed = jnp.pad(packed, ((0, 0), (0, LANES - packed.shape[1])))
    own = (jnp.arange(SLICES, dtype=jnp.int32) == me)[:, None, None]
    spare = jnp.where(own, packed[None], jnp.zeros((), bf16)).reshape(n_dev, 1, 1, LANES)
    spare = jnp.pad(spare, ((0, 0), (0, 0), (0, slots - tiles - 1), (0, 0)))
    extra = jnp.concatenate([extra, spare], axis=2)
    sent = jnp.concatenate([main, extra], axis=1)
    back = routed(sent)

    up_term = contract(x_rows, g_all, ((0,), (0,))).astype(bf16)
    got_up = ring(y_block(up_term, 2), 1)
    sums = replica_sum(up_term, down_term, got_up, got_down)

    main = back[:, :tiles].reshape(experts, SLICES, tiles, slots, LANES)
    main = main.transpose(0, 3, 1, 2, 4).reshape(experts * slots, model_width)
    extra = back[:, tiles, :tiles].reshape(experts, model_width)
    table = jnp.concatenate([main, extra], axis=0)
    grad_tokens = contract(pick, table, ((0,), (0,))).astype(bf16)
    spare = back[:, tiles, tiles].astype(f32).reshape(experts, SLICES, LANES).sum(axis=1)
    spare = spare[:, : 3 * (slots + 1)].reshape(experts, 3, slots + 1).sum(axis=1)
    flat = jnp.concatenate([spare[:, :slots].reshape(-1), spare[:, slots]])
    hit = main_pos[:, None] == jnp.arange(rows, dtype=jnp.int32)[None, :]
    grad_gates = jnp.sum(jnp.where(hit, flat[None, :], 0.0), axis=1, keepdims=True) / gates
    return grad_tokens, grad_gates, sums[:, :hidden], sums[:, hidden:]


def solution(mesh):
    token_spec, weight_spec = P(("rep", "exp"), None), P(("exp", "rep"), None)
    return jax.shard_map(
        shards,
        mesh=mesh,
        in_specs=(token_spec,) * 4 + (weight_spec,) * 2,
        out_specs=(token_spec, token_spec, weight_spec, weight_spec),
        check_vma=False,
    )
```

```python
import jax
import jax.numpy as jnp
from jax import lax
from jax.sharding import PartitionSpec as P


SLICES = 4
LANES = 128
Z_BLOCKS = 4
BOTH = ("rep", "exp")


def contract(left, right, dims):
    return lax.dot_general(
        left, right, ((dims[0], dims[1]), ((), ())), preferred_element_type=jnp.float32
    )


def split3(x):
    first = x.astype(jnp.bfloat16)
    rest = x - first.astype(jnp.float32)
    second = rest.astype(jnp.bfloat16)
    third = (rest - second.astype(jnp.float32)).astype(jnp.bfloat16)
    return first, second, third


def moved(x, n_rep, n_exp, where, shift=0):
    pairs = []
    for rep in range(n_rep):
        for exp in range(n_exp):
            y, core, base, far, near = rep // 2, rep % 2, exp // 4 * 4, exp // 2 % 2, exp % 2
            core, far, near = where(core, far, near)
            y = (y + shift) % (n_rep // 2)
            pairs.append((rep * n_exp + exp, (y * 2 + core) * n_exp + base + far * 2 + near))
    return lax.ppermute(x, BOTH, pairs)


def shards(tokens, cotangent, gates, routes, w_up, w_down_t):
    tok_dev, model_width = tokens.shape
    piece = model_width // SLICES
    tiles = piece // LANES
    n_rep, n_dev = lax.axis_size("rep"), lax.axis_size("exp")
    experts = n_dev // SLICES
    slots = 8
    quarter = n_dev // SLICES
    per_quarter = quarter * (slots + 1)
    hidden = w_up.shape[1]
    bf16, f32 = jnp.bfloat16, jnp.float32
    core, far, near = lax.axis_index("rep") % 2, lax.axis_index("exp") // 2 % 2, lax.axis_index("exp") % 2
    me = core * 2 + near
    token_groups = [
        [
            (y * 2 + c) * n_dev + e * SLICES + (k ^ e % Z_BLOCKS // 2) * 2 + b
            for e in range(experts)
            for c in range(2)
            for b in range(2)
        ]
        for y in range(n_rep // 2)
        for k in range(2)
    ]

    y_now, y_size = lax.axis_index("rep") // 2, n_rep // 2

    def ring(x, step):
        return moved(x, n_rep, n_dev, lambda c, h, b: (c, h, b), step)

    def gathered_weights(own_up, own_down):
        own = jnp.concatenate([own_up, own_down], axis=0)
        half = own_up.shape[0]
        left, right = ring(own, 1), ring(own, -1)
        far_up, far_down = ring(left[:half], 1), ring(right[half:], -1)

        def placed(blocks):
            twice = jnp.concatenate(blocks + blocks, axis=0)
            start = (y_size - y_now) * half
            return lax.dynamic_slice_in_dim(twice, start, y_size * half, axis=0)

        return (
            placed([own_up, right[:half], far_up, left[:half]]),
            placed([own_down, right[half:], far_down, left[half:]]),
        )

    def y_block(term, step):
        rows_y = term.shape[0] // y_size
        start = (y_now + step) % y_size * rows_y
        return lax.dynamic_slice_in_dim(term, start, rows_y, axis=0)

    def plus(part, got):
        return (part.astype(f32) + got.astype(f32)).astype(bf16)

    def replica_sum(up_term, down_term, got_up, got_down):
        ahead = jnp.concatenate([plus(y_block(up_term, 1), got_up), y_block(down_term, 1)], axis=1)
        behind = jnp.concatenate(
            [y_block(up_term, 3), plus(y_block(down_term, 3), got_down)], axis=1
        )
        from_left, from_right = ring(ahead, 1), ring(behind, -1)
        total = jnp.concatenate([y_block(up_term, 0), y_block(down_term, 0)], axis=1).astype(f32)
        total = (total + from_left.astype(f32) + from_right.astype(f32)).astype(bf16)
        half = total.shape[0] // 2
        low, high = total[:half], total[half:]
        first, second = jnp.where(far == 1, high, low), jnp.where(far == 1, low, high)
        first = moved(first, n_rep, n_dev, lambda c, h, b: (h, c, b))
        second = moved(second, n_rep, n_dev, lambda c, h, b: (1 - h, c, b))
        return first.astype(f32) + second.astype(f32)

    def routed(x):
        return lax.all_to_all(
            x, BOTH, split_axis=0, concat_axis=0, axis_index_groups=token_groups, tiled=True
        )

    def other_core(x):
        return moved(x, n_rep, n_dev, lambda c, h, b: (1 - c, h, b))

    def other_near(x):
        return moved(x, n_rep, n_dev, lambda c, h, b: (c, h, 1 - b))

    both = jnp.concatenate([w_up, w_down_t], axis=0)
    first = moved(both, n_rep, n_dev, lambda c, h, b: (h, c, b))
    second = moved(both, n_rep, n_dev, lambda c, h, b: (h, 1 - c, b))
    part = w_up.shape[0]

    def paired(rows):
        ones, twos = first[rows], second[rows]
        return jnp.where(
            far == 0, jnp.concatenate([ones, twos], axis=0), jnp.concatenate([twos, ones], axis=0)
        )

    own_up = paired(slice(0, part))
    own_down = paired(slice(part, 2 * part))
    up, down = gathered_weights(own_up, own_down)

    route = routes.reshape(-1)
    order = jnp.arange(tok_dev, dtype=jnp.int32)
    same = (route[:, None] == route[None, :]) & (order[None, :] < order[:, None])
    slot = jnp.sum(same.astype(jnp.int32), axis=1)
    main_pos = jnp.where(slot < slots, route * slots + slot, experts * slots + route)
    rows = experts * (slots + 1)
    pick = (main_pos[None, :] == jnp.arange(rows, dtype=jnp.int32)[:, None]).astype(bf16)

    def packed_rows(values):
        table = contract(pick, values, ((1,), (0,))).astype(bf16)
        main = table[: experts * slots].reshape(experts, slots, SLICES, tiles, LANES)
        main = main.transpose(0, 2, 3, 1, 4).reshape(n_dev, tiles, slots, LANES)
        extra = table[experts * slots :].reshape(n_dev, 1, tiles, LANES)
        extra = jnp.pad(extra, ((0, 0), (0, 0), (0, slots - tiles), (0, 0)))
        return [main, extra]

    def unpack(got):
        main = got[:, :tiles].transpose(0, 2, 1, 3).reshape(SLICES, quarter * slots, piece)
        extra = got[:, tiles, :tiles].reshape(SLICES, quarter, piece)
        both = jnp.concatenate([main, extra], axis=1)
        blocks = [
            lax.dynamic_index_in_dim(both, me ^ d, axis=0, keepdims=False) for d in range(SLICES)
        ]
        return jnp.concatenate(blocks, axis=0)

    def reduced(rows_in, matrix):
        theirs = contract(rows_in[2 * per_quarter :], matrix, ((1,), (0,))).astype(bf16)
        theirs = other_core(theirs)
        mine = contract(rows_in[: 2 * per_quarter], matrix, ((1,), (0,)))
        ours = (mine + theirs.astype(f32)).astype(bf16)
        passed = other_near(ours)
        passed = jnp.concatenate([passed[per_quarter:], passed[:per_quarter]], axis=0)
        return ours.astype(f32) + passed.astype(f32)

    def gathered(pair):
        return jnp.concatenate([pair, other_core(pair)], axis=0)

    out_grad = (gates * cotangent.astype(f32)).astype(bf16)
    sent = jnp.concatenate(packed_rows(tokens) + packed_rows(out_grad), axis=1)
    got = routed(sent)
    x_rows = unpack(got[:, : tiles + 1])
    d_rows = unpack(got[:, tiles + 1 :])

    activation = reduced(x_rows, up)
    hidden_grad = reduced(d_rows, down)
    gating = jax.nn.sigmoid(activation)
    hidden_act = (activation * gating).astype(bf16)
    hidden_act, activation = lax.optimization_barrier((hidden_act, activation))
    gating = jax.nn.sigmoid(activation)
    h_all = gathered(hidden_act)
    down_term = contract(d_rows, h_all, ((0,), (0,))).astype(bf16)
    got_down = ring(y_block(down_term, 2), -1)
    act_grad = (hidden_grad * gating * (1.0 + activation * (1.0 - gating))).astype(bf16)
    dots = jnp.sum((hidden_act.astype(f32) * hidden_grad)[:per_quarter], axis=1)
    g_all = gathered(act_grad)

    dx = contract(g_all, up, ((1,), (1,))).astype(bf16).reshape(SLICES, per_quarter, piece)
    dx = jnp.stack(
        [lax.dynamic_index_in_dim(dx, me ^ d, axis=0, keepdims=False) for d in range(SLICES)]
    )
    main = dx[:, : quarter * slots].reshape(n_dev, slots, tiles, LANES).transpose(0, 2, 1, 3)
    extra = dx[:, quarter * slots :].reshape(n_dev, 1, tiles, LANES)
    per_source = jnp.concatenate(
        [dots[: quarter * slots].reshape(quarter, slots), dots[quarter * slots :][:, None]], axis=1
    )
    packed = jnp.concatenate(split3(per_source), axis=1)
    packed = jnp.pad(packed, ((0, 0), (0, LANES - packed.shape[1])))
    own = (jnp.arange(SLICES, dtype=jnp.int32) == me)[:, None, None]
    spare = jnp.where(own, packed[None], jnp.zeros((), bf16)).reshape(n_dev, 1, 1, LANES)
    spare = jnp.pad(spare, ((0, 0), (0, 0), (0, slots - tiles - 1), (0, 0)))
    extra = jnp.concatenate([extra, spare], axis=2)
    sent = jnp.concatenate([main, extra], axis=1)
    back = routed(sent)

    up_term = contract(x_rows, g_all, ((0,), (0,))).astype(bf16)
    got_up = ring(y_block(up_term, 2), 1)
    sums = replica_sum(up_term, down_term, got_up, got_down)

    main = back[:, :tiles].reshape(experts, SLICES, tiles, slots, LANES)
    main = main.transpose(0, 3, 1, 2, 4).reshape(experts * slots, model_width)
    extra = back[:, tiles, :tiles].reshape(experts, model_width)
    table = jnp.concatenate([main, extra], axis=0)
    grad_tokens = contract(pick, table, ((0,), (0,))).astype(bf16)
    spare = back[:, tiles, tiles].astype(f32).reshape(experts, SLICES, LANES).sum(axis=1)
    spare = spare[:, : 3 * (slots + 1)].reshape(experts, 3, slots + 1).sum(axis=1)
    flat = jnp.concatenate([spare[:, :slots].reshape(-1), spare[:, slots]])
    hit = main_pos[:, None] == jnp.arange(rows, dtype=jnp.int32)[None, :]
    grad_gates = jnp.sum(jnp.where(hit, flat[None, :], 0.0), axis=1, keepdims=True) / gates
    return grad_tokens, grad_gates, sums[:, :hidden], sums[:, hidden:]


def solution(mesh):
    token_spec, weight_spec = P(("rep", "exp"), None), P(("exp", "rep"), None)
    return jax.shard_map(
        shards,
        mesh=mesh,
        in_specs=(token_spec,) * 4 + (weight_spec,) * 2,
        out_specs=(token_spec, token_spec, weight_spec, weight_spec),
        check_vma=False,
    )
```
